32 devices in a mesh: front: 4 (over y, x), row: 4 (over z), col: 2 (over core).
Axes of the slice: x: 2, y: 2, z: 4, core: 2. Of those that a mesh axis runs over, the one named last changes fastest.
Arguments:
- front_in: float32 [32768, 8192], P(('front', 'row'), 'col'), parts along dimension 0, may hold values from -6 to 6
- child_tiles: bfloat16 [32, 56, 128, 128], P(('front', 'row', 'col')), parts along dimension 0, may hold values from -6 to 6
- child_map: int32 [32, 56], P(('front', 'row', 'col')), parts along dimension 0, may hold values from 0 to 4095, as said below
- pattern: int32 [256, 64], P('front'), parts along dimension 0, may hold values 0 or 1
- pivot_inverse: float32 [8, 512, 512], P('front'), parts along dimension 0, may hold values from -0.01171875 to 0.01171875
Outputs:
- front_out: float32 [32768, 8192], P(('front', 'row'), 'col'), parts along dimension 0
The draws below stay inside these ranges and needn't reach their ends.
There are 4 independent parts, one for each index of `front`. The reference program is written for one: setup_inputs(seed, part) draws one part's arguments, and reference() takes and returns one part's arrays. A program takes and returns all parts, laid end to end along the dimension named above; each array names one. Nothing has to cross between parts.
Inputs may be any that keep to these rules, and one draw needn't show every extreme that they name: Entries j * 7 to (j + 1) * 7 - 1 of each row of child_map name tiles held by device j of the front's grid, j = grid row * 2 + grid column, that device holding tile rows of its 2048 rows and tile columns of its 4096 columns.
All inputs are finite; a program needn't handle non-finite values.
Results may differ from the reference program's by a relative error of at most 0.0062.
Values may be sent and summed in bfloat16 or wider, within the bound.
No kernel may reach another device: no remote copies, remote signals or barrier semaphores. Data moves between devices by JAX's collectives and lax.ppermute only.
A program may use at most 256 MiB of HBM per device.

```python
import jax
import jax.numpy as jnp
from jax import lax

ORDER = 8192
TILE = 128
PANEL = 512
PANELS = 2
SLOTS = 7
NT = 64
GRID_ROWS = 4
GRID_COLS = 2
GROUPS = 8


def draw_child_map(key, part):
    groups = GRID_ROWS * GRID_COLS
    tile_rows = NT // GRID_ROWS
    tile_cols = NT // GRID_COLS
    local_tile = jax.random.randint(key, (groups, groups, SLOTS), 0, tile_rows * tile_cols)
    local_tile = local_tile.at[0, :, 0].set(0)
    local_tile = local_tile.at[groups - 1, :, SLOTS - 1].set(tile_rows * tile_cols - 1)
    target = jnp.arange(groups)[None, :, None]
    grid_row = target // GRID_COLS * tile_rows + local_tile // tile_cols
    grid_col = target % GRID_COLS * tile_cols + local_tile % tile_cols
    return (grid_row * NT + grid_col).reshape(groups, groups * SLOTS).astype(jnp.int32)


def plant(drawn, rng, least, largest):
    extent = drawn.shape
    place = [jax.random.randint(jax.random.fold_in(rng, axis), (), 0, extent[axis]) for axis in range(len(extent))]
    drawn = drawn.at[tuple(place)].set(least)
    longest = extent.index(max(extent))
    place[longest] = (place[longest] + 1) % extent[longest]
    return drawn.at[tuple(place)].set(largest)


def level_of(stream_key, shape, split, least, top_value):
    gain = 1.0
    for position, blocks in split:
        draws = jax.random.uniform(jax.random.fold_in(jax.random.fold_in(stream_key, 6), position), (blocks,), jnp.float32, least / len(split), top_value / len(split))
        gain = gain * jnp.repeat(jnp.exp(draws), shape[position] // blocks).reshape((-1,) + (1,) * (len(shape) - 1 - position))
    return gain


def normal_values(stream_key, dims, width, limit, pieces=(), dtype=jnp.bfloat16):
    gain = level_of(stream_key, dims, pieces, -0.22, 0.18) if pieces else 1.0
    entries = jax.random.normal(stream_key, dims, jnp.float32) * width * gain
    return jnp.minimum(jnp.maximum(entries, -limit), limit).astype(dtype)


def setup_inputs(seed: int = 0, part: int = 0) -> dict:
    keys = jax.random.split(jax.random.key(seed), 6)
    part_keys = jax.random.split(jax.random.fold_in(keys[5], part), 6)
    return {
        "front_in": normal_values(part_keys[0], (ORDER, ORDER), 1.0, 6.0, ((0, 4), (1, 2)), jnp.float32),
        "child_tiles": normal_values(part_keys[1], (GROUPS, GROUPS * SLOTS, TILE, TILE), 1.0, 6.0, ((0, 8),)),
        "child_map": draw_child_map(jax.random.fold_in(jax.random.fold_in(keys[5], part), 71), part),
        "pattern": plant((jax.random.randint(part_keys[3], (NT, NT), 0, 4) < 3).astype(jnp.int32), jax.random.fold_in(part_keys[3], 1), 0, 1),
        "pivot_inverse": normal_values(part_keys[4], (PANELS, PANEL, PANEL), (PANEL * PANEL) ** -0.5, 0.01171875, (), jnp.float32),
    }


def reference(front_in, child_tiles, child_map, pattern, pivot_inverse):
    child_flat = child_tiles.reshape(-1, TILE, TILE).astype(jnp.float32)
    target = child_map.reshape(-1).astype(jnp.int32)
    grid_row = target // NT
    grid_col = target % NT
    matrix = front_in.reshape(NT, TILE, NT, TILE).at[grid_row, :, grid_col, :].add(child_flat).reshape(ORDER, ORDER)
    for panel_index in range(PANELS):
        first_col = panel_index * PANEL
        finish = first_col + PANEL
        lower_part = jnp.dot(matrix[finish:, first_col:finish], pivot_inverse[panel_index], precision=lax.Precision.HIGHEST, preferred_element_type=jnp.float32)
        upper_rows = matrix[first_col:finish, finish:].astype(jnp.bfloat16)
        update = jnp.dot(lower_part.astype(jnp.bfloat16), upper_rows, preferred_element_type=jnp.float32)
        tile_mask = pattern[finish // TILE:, finish // TILE:].astype(jnp.float32)
        count = NT - finish // TILE
        update = (update.reshape(count, TILE, count, TILE) * tile_mask[:, None, :, None]).reshape(count * TILE, count * TILE)
        matrix = matrix.at[finish:, finish:].add(-update)
        matrix = matrix.at[finish:, first_col:finish].set(lower_part)
    return matrix
```

```python
import functools

import jax
import jax.numpy as jnp
from jax import lax
from jax.experimental import pallas as pl
from jax.experimental.pallas import tpu as pltpu
from jax.sharding import PartitionSpec as P


F32 = jnp.float32
BF16 = jnp.bfloat16
ANY = pl.BlockSpec(memory_space=pl.ANY)


def cost(flops, nbytes):
    return pl.CostEstimate(flops=int(flops), bytes_accessed=int(nbytes), transcendentals=0)


def load_kids(kid_refs, kids, sems):
    slots = kid_refs[0].shape[0]
    copies = [
        pltpu.make_async_copy(ref, kids.at[pl.ds(g * slots, slots)], sems.at[g])
        for g, ref in enumerate(kid_refs)
    ]
    for copy in copies:
        copy.start()
    for copy in copies:
        copy.wait()


def add_kids(acc, rows, cols, tile, head, following, kids):
    first = head[tile]

    @pl.when(first >= 0)
    def _():
        def step(i):
            acc[rows, cols] += kids[i].astype(F32)
            return following[i]

        lax.while_loop(lambda i: i >= 0, step, first)


def assemble(front, kid_list, head, following, row_blocks, height, col_block, width, out_type):
    col_count = front.shape[1]
    groups = len(kid_list)
    slots, tile = kid_list[0].shape[:2]
    per_row = col_count // tile
    direct = out_type == F32

    def kernel(head, following, x_ref, *rest):
        kid_refs, (o_ref, kids, sems, *scratch) = rest[:groups], rest[groups:]
        step = pl.program_id(0)

        @pl.when(step == 0)
        def _():
            load_kids(kid_refs, kids, sems)

        acc = o_ref if direct else scratch[0]
        acc[...] = x_ref[...]
        for r in range(height // tile):
            for c in range(width // tile):
                add_kids(
                    acc,
                    slice(r * tile, (r + 1) * tile),
                    slice(c * tile, (c + 1) * tile),
                    (step * (height // tile) + r) * per_row + col_block * (width // tile) + c,
                    head,
                    following,
                    kids,
                )
        if not direct:
            o_ref[...] = acc[...].astype(out_type)

    size = row_blocks * height * width
    return pl.pallas_call(
        kernel,
        out_shape=jax.ShapeDtypeStruct((row_blocks * height, width), out_type),
        grid_spec=pltpu.PrefetchScalarGridSpec(
            num_scalar_prefetch=2,
            grid=(row_blocks,),
            in_specs=[pl.BlockSpec((height, width), lambda i, *_: (i, col_block))] + [ANY] * groups,
            out_specs=pl.BlockSpec((height, width), lambda i, *_: (i, 0)),
            scratch_shapes=[
                pltpu.VMEM((groups * slots, tile, tile), BF16),
                pltpu.SemaphoreType.DMA((groups,)),
            ]
            + ([] if direct else [pltpu.VMEM((height, width), F32)]),
        ),
        cost_estimate=cost(size, size * 8),
        name="assemble",
    )(head, following, front, *kid_list)


def first_lower(matrix, inverse, row_base, panel):
    row_count = matrix.shape[0]
    height = 256

    def kernel(base, a_ref, p_ref, out_ref, low_ref):
        a = a_ref[...]
        low = jnp.dot(a, p_ref[0], precision=lax.Precision.HIGHEST, preferred_element_type=F32)
        below = base[0] + pl.program_id(0) * height + lax.broadcasted_iota(jnp.int32, low.shape, 0) >= panel
        out_ref[...] = jnp.where(below, low, a)
        low_ref[...] = jnp.where(below, low, 0.0).astype(BF16)

    return pl.pallas_call(
        kernel,
        out_shape=(
            jax.ShapeDtypeStruct((row_count, panel), F32),
            jax.ShapeDtypeStruct((row_count, panel), BF16),
        ),
        grid_spec=pltpu.PrefetchScalarGridSpec(
            num_scalar_prefetch=1,
            grid=(row_count // height,),
            in_specs=[
                pl.BlockSpec((height, panel), lambda i, *_: (i, 0)),
                pl.BlockSpec((1, panel, panel), lambda i, *_: (0, 0, 0)),
            ],
            out_specs=(
                pl.BlockSpec((height, panel), lambda i, *_: (i, 0)),
                pl.BlockSpec((height, panel), lambda i, *_: (i, 0)),
            ),
        ),
        cost_estimate=cost(12 * row_count * panel * panel, row_count * panel * 10),
        name="lower0",
    )(row_base, matrix, inverse)


def masked_update(acc, product, mask, first_row, first_col, tile, out_ref):
    for r in range(product.shape[0] // tile):
        for c in range(product.shape[1] // tile):
            kept = mask[first_row + r, first_col + c].astype(F32)
            rows, cols = slice(r * tile, (r + 1) * tile), slice(c * tile, (c + 1) * tile)
            out_ref[rows, cols] = (acc[rows, cols] - product[rows, cols] * kept).astype(out_ref.dtype)


def fetch(place, candidates, scratch, sem, columns=None):
    for r, ref in enumerate(candidates):
        source = ref if columns is None else ref.at[:, columns]

        @pl.when(place[0] == r)
        def _():
            copy = pltpu.make_async_copy(source, scratch, sem)
            copy.start()
            copy.wait()


def second_lower(matrix, inverse, lower, uppers, mask, row_base, place, panel, tile):
    row_count = matrix.shape[0]
    height = 256
    count = len(uppers)

    def kernel(base, place, mask, a_ref, p_ref, l_ref, *rest):
        u_refs, (out_ref, low_ref, upper, current, sem) = rest[:count], rest[count:]
        step = pl.program_id(0)

        @pl.when(step == 0)
        def _():
            fetch(place, u_refs, upper, sem)

        product = jnp.dot(l_ref[...], upper[...], preferred_element_type=F32)
        masked_update(a_ref, product, mask, step * (height // tile), panel // tile, tile, current)
        now = current[...]
        low = jnp.dot(now, p_ref[0], precision=lax.Precision.HIGHEST, preferred_element_type=F32)
        below = base[0] + step * height + lax.broadcasted_iota(jnp.int32, low.shape, 0) >= 2 * panel
        out_ref[...] = jnp.where(below, low, now)
        low_ref[...] = jnp.where(below, low, 0.0).astype(BF16)

    return pl.pallas_call(
        kernel,
        out_shape=(
            jax.ShapeDtypeStruct((row_count, panel), F32),
            jax.ShapeDtypeStruct((row_count, panel), BF16),
        ),
        grid_spec=pltpu.PrefetchScalarGridSpec(
            num_scalar_prefetch=3,
            grid=(row_count // height,),
            in_specs=[
                pl.BlockSpec((height, panel), lambda i, *_: (i, 1)),
                pl.BlockSpec((1, panel, panel), lambda i, *_: (1, 0, 0)),
                pl.BlockSpec((height, panel), lambda i, *_: (i, 0)),
            ]
            + [ANY] * count,
            out_specs=(
                pl.BlockSpec((height, panel), lambda i, *_: (i, 0)),
                pl.BlockSpec((height, panel), lambda i, *_: (i, 0)),
            ),
            scratch_shapes=[
                pltpu.VMEM((panel, panel), BF16),
                pltpu.VMEM((height, panel), F32),
                pltpu.SemaphoreType.DMA,
            ],
        ),
        cost_estimate=cost(14 * row_count * panel * panel, row_count * panel * 12),
        name="lower1",
    )(row_base, place, mask, matrix, inverse, lower, *uppers)


def second_upper(matrix, lower, upper, upper_start, start, width, mask, panel, tile):
    height = 256
    blocks = panel // height
    offset = (start - upper_start) // width

    def kernel(mask, a_ref, l_ref, u_ref, out_ref):
        product = jnp.dot(l_ref[...], u_ref[...], preferred_element_type=F32)
        first_row = panel // tile + pl.program_id(0) * (height // tile)
        masked_update(a_ref, product, mask, first_row, start // tile, tile, out_ref)

    return pl.pallas_call(
        kernel,
        out_shape=jax.ShapeDtypeStruct((panel, width), BF16),
        grid_spec=pltpu.PrefetchScalarGridSpec(
            num_scalar_prefetch=1,
            grid=(blocks,),
            in_specs=[
                pl.BlockSpec((height, width), lambda i, *_: (blocks + i, start // width)),
                pl.BlockSpec((height, panel), lambda i, *_: (blocks + i, 0)),
                pl.BlockSpec((panel, width), lambda i, *_: (0, offset)),
            ],
            out_specs=pl.BlockSpec((height, width), lambda i, *_: (i, 0)),
        ),
        cost_estimate=cost(2 * panel * panel * width, panel * width * 8),
        name="upper1",
    )(mask, matrix, lower, upper)


def finish(matrix, lowers, pieces, start, width, mask, place, panel, tile, stored):
    row_count = matrix.shape[0]
    height = 256
    counts = [len(candidates) for candidates, _ in pieces]
    flat = [ref for candidates, _ in pieces for ref in candidates]
    special = [] if stored is None else [stored]

    def kernel(place, mask, a_ref, l0_ref, l1_ref, *rest):
        extra, rest = rest[: len(special)], rest[len(special) :]
        refs, (out_ref, upper, sems) = rest[: len(flat)], rest[len(flat) :]
        step = pl.program_id(0)

        @pl.when(step == 0)
        def _():
            at = 0
            for k, (count, (_, first)) in enumerate(zip(counts, pieces)):
                fetch(
                    place,
                    refs[at : at + count],
                    upper.at[k],
                    sems.at[k],
                    slice(start - first, start - first + width),
                )
                at += count

        def update():
            product = jnp.dot(l0_ref[...], upper[0], preferred_element_type=F32)
            product += jnp.dot(l1_ref[...], upper[1], preferred_element_type=F32)
            masked_update(a_ref, product, mask, step * (height // tile), start // tile, tile, out_ref)

        if special:
            pl.when(place[1] != 0)(update)

            @pl.when(place[1] == 0)
            def _():
                out_ref[...] = extra[0][...]
        else:
            update()

    return pl.pallas_call(
        kernel,
        out_shape=jax.ShapeDtypeStruct(matrix.shape, F32),
        grid_spec=pltpu.PrefetchScalarGridSpec(
            num_scalar_prefetch=2,
            grid=(row_count // height,),
            in_specs=[
                pl.BlockSpec((height, width), lambda i, *_: (i, start // width)),
                pl.BlockSpec((height, panel), lambda i, *_: (i, 0)),
                pl.BlockSpec((height, panel), lambda i, *_: (i, 0)),
            ]
            + [pl.BlockSpec((height, width), lambda i, *_: (i, 0)) for _ in special]
            + [ANY] * len(flat),
            out_specs=pl.BlockSpec((height, width), lambda i, *_: (i, start // width)),
            scratch_shapes=[
                pltpu.VMEM((2, panel, width), BF16),
                pltpu.SemaphoreType.DMA((2,)),
            ],
        ),
        input_output_aliases={2: 0},
        cost_estimate=cost(4 * row_count * panel * width, row_count * width * 8),
        name="finish",
    )(place, mask, matrix, *lowers, *special, *flat)


def over_cols(x):
    count = lax.axis_size("col")
    mine = lax.axis_index("col")
    reach = 1
    while reach < count:
        pairs = [(i, i + reach) for i in range(min(reach, count - reach))]
        got = lax.ppermute(x, "col", pairs)
        x = jnp.where(mine < reach, x, got)
        reach *= 2
    return x


def down_rows(x, skip_first):
    rows, cols = lax.axis_size("row"), lax.axis_size("col")
    held = [x]
    for r in range(rows - 1):
        pairs = [(r * cols + c, (r + 1) * cols + c) for c in range(1 if skip_first else 0, cols)]
        held.append(lax.ppermute(held[-1], ("row", "col"), pairs))
    return held


def body(front_in, child_tiles, child_map, pattern, pivot_inverse):
    row_count, col_count = front_in.shape
    tile = child_tiles.shape[-1]
    panel = pivot_inverse.shape[1]
    side = pattern.shape[1]
    grid_rows, grid_cols = lax.axis_size("row"), lax.axis_size("col")
    groups = grid_rows * grid_cols
    slots = child_map.shape[1] // groups
    row_index, col_index = lax.axis_index("row"), lax.axis_index("col")
    me = row_index * grid_cols + col_index
    tile_rows, tile_cols = row_count // tile, col_count // tile

    outgoing = child_tiles.reshape(groups, slots, tile, tile)
    kid_list = []
    for k in range(groups):
        mine = lax.dynamic_index_in_dim(outgoing, me ^ k, 0, False)
        pairs = [(i, i ^ k) for i in range(groups)]
        kid_list.append(mine if k == 0 else lax.ppermute(mine, ("row", "col"), pairs))
    placed = lax.all_to_all(
        child_map.reshape(groups, slots), ("row", "col"), split_axis=0, concat_axis=0, tiled=True
    )
    targets = placed[me ^ jnp.arange(groups)].reshape(-1)
    local = (targets // side - row_index * tile_rows) * tile_cols + (
        targets % side - col_index * tile_cols
    )
    order = jnp.arange(local.shape[0])
    none = jnp.int32(local.shape[0])
    head = jnp.min(
        jnp.where(local[None, :] == jnp.arange(tile_rows * tile_cols)[:, None], order[None, :], none), axis=1
    )
    head = jnp.where(head == none, -1, head).astype(jnp.int32)
    later = (local[None, :] == local[:, None]) & (order[None, :] > order[:, None])
    following = jnp.min(jnp.where(later, order[None, :], none), axis=1)
    following = jnp.where(following == none, -1, following).astype(jnp.int32)

    mask = lax.dynamic_slice(
        pattern, (row_index * tile_rows, col_index * tile_cols), (tile_rows, tile_cols)
    )
    place = jnp.stack([row_index, col_index]).astype(jnp.int32)
    row_base = (row_index * row_count).astype(jnp.int32).reshape(1)

    wide = 2 * panel
    first_pieces = [(panel, 2 * panel)]
    first_pieces += [(s, s + wide) for s in range(2 * panel, col_count, wide)]
    first_pieces += [(0, panel)]
    upper0 = {}
    for s, e in first_pieces:
        own = assemble(
            front_in, kid_list, head, following, panel // tile, tile, s // (e - s), e - s, BF16
        )
        upper0[s, e] = down_rows(own, s == 0)

    matrix = assemble(
        front_in, kid_list, head, following, row_count // (2 * tile), 2 * tile, 0, col_count, F32
    )
    panel0, lower0 = first_lower(matrix, pivot_inverse, row_base, panel)
    lower0 = over_cols(lower0)

    second_pieces = [(0, panel), (panel, 2 * panel)]
    second_pieces += [(s, s + wide) for s in range(2 * panel, col_count, wide)]
    if col_count > 2 * panel:
        s, e = second_pieces.pop()
        q = panel // 2
        second_pieces += [(s, s + panel), (s + panel, s + panel + q), (s + panel + q, e)]

    def around(s):
        return next((a, b) for a, b in first_pieces if a <= s < b)

    upper1 = {}
    for s, e in second_pieces:
        a, b = around(s)
        upper1[s, e] = second_upper(matrix, lower0, upper0[a, b][0], a, s, e - s, mask, panel, tile)
    panel1, lower1 = second_lower(
        matrix, pivot_inverse, lower0, upper0[panel, 2 * panel], mask, row_base, place, panel, tile
    )
    lower1 = over_cols(lower1)
    matrix, upper1 = lax.optimization_barrier((matrix, upper1))
    for s, e in second_pieces:
        a, b = around(s)
        pieces = [(upper0[a, b], a), (down_rows(upper1[s, e], s < 2 * panel), s)]
        stored = {0: panel0, panel: panel1}.get(s)
        matrix = finish(
            matrix, [lower0, lower1], pieces, s, e - s, mask, place, panel, tile, stored
        )
    return matrix


def solution(mesh):
    placed = (
        P(("front", "row"), "col"),
        P(("front", "row", "col"), None, None, None),
        P(("front", "row", "col"), None),
        P("front", None),
        P("front", None, None),
    )
    return jax.shard_map(
        body, mesh=mesh, in_specs=placed, out_specs=P(("front", "row"), "col"), check_vma=False
    )
```
